32 devices in a mesh: member: 8 (over z, x), space: 4 (over y, core).
Axes of the slice: x: 2, y: 2, z: 4, core: 2. Of those that a mesh axis runs over, the one named last changes fastest.
Arguments:
- states: float32 [1024, 24576], P('member', 'space'), may hold values from -6 to 6
- obs_values: float32 [2, 2048], replicated, may hold values from -6 to 6
- obs_weights: float32 [2, 2048], replicated, may hold values from 0.2 to 2
- obs_cell: int32 [2, 4, 4], P(None, 'space'), may hold values from 0 to 47
- op_select: int32 [2, 4, 4], P(None, 'space'), may hold values from 0 to 7
- op_table: float32 [8, 128, 128], replicated, may hold values from -0.5 to 0.5
- loc_obs: int32 [2, 4, 48, 8], P(None, 'space', 'member'), may hold values from 0 to 11
- loc_tile: int32 [2, 4, 48, 8], P(None, 'space', 'member'), may hold values from 0 to 7
- loc_tiles: float32 [8, 128, 128], replicated, may hold values from 0 to 1
Outputs:
- analysis: float32 [1024, 24576], P('member', 'space')
The draws below stay inside these ranges and needn't reach their ends.
All inputs are finite; a program needn't handle non-finite values.
Results may differ from the reference program's by a relative error of at most 0.00012.
Values sent between devices are 32-bit elements; how exact they have to be, the bound alone decides.
A program may use at most 128 MiB of HBM per device.

```python
import math
import jax
import jax.numpy as jnp
from jax import lax

K = 1024
BLK = 128
OB = 4
LOC = 8
NH = 8
NT = 8
BATCHES = 2
NB = 48
NCELLS = 24576
NOB = 16
N_SPACE = 4


def plant(entries, stream_key, smallest, largest):
    shape = entries.shape
    place = [jax.random.randint(jax.random.fold_in(stream_key, axis), (), 0, shape[axis]) for axis in range(len(shape))]
    entries = entries.at[tuple(place)].set(smallest)
    longest = shape.index(max(shape))
    place[longest] = (place[longest] + 1) % shape[longest]
    return entries.at[tuple(place)].set(largest)


def block_levels(stream_key, dims, shards, smallest, largest):
    def one(axis_at, blocks):
        heights = jax.random.uniform(jax.random.fold_in(jax.random.fold_in(stream_key, 6), axis_at), (blocks,), jnp.float32, smallest / len(shards), largest / len(shards))
        return jnp.repeat(jnp.exp(heights), dims[axis_at] // blocks).reshape((-1,) + (1,) * (len(dims) - axis_at - 1))

    level = one(*shards[0])
    for cut in shards[1:]:
        level = level * one(*cut)
    return level


def scatter_about(stream_key, extent, scale, bound, shards=(), dtype=jnp.bfloat16):
    factor_of = block_levels(stream_key, extent, shards, -0.22, 0.18) if shards else 1.0
    entries = jax.random.normal(stream_key, extent, jnp.float32) * scale * factor_of
    return jnp.minimum(jnp.maximum(entries, -bound), bound).astype(dtype)


def setup_inputs(seed: int = 0) -> dict:
    splits = jax.random.split(jax.random.key(seed), 10)
    return {
        "states": scatter_about(splits[0], (K, NCELLS), 1.0, 6.0, ((0, 8), (1, 4)), jnp.float32),
        "obs_values": scatter_about(splits[1], (BATCHES, NOB * BLK), 1.0, 6.0, (), jnp.float32),
        "obs_weights": jnp.clip(jnp.exp(jax.random.uniform(splits[2], (BATCHES, NOB * BLK), jnp.float32, math.log(0.2), math.log(2.0))), 0.2, 2.0),
        "obs_cell": plant(jax.random.randint(splits[3], (BATCHES, N_SPACE, OB), 0, NB), jax.random.fold_in(splits[3], 1), 0, NB - 1).astype(jnp.int32),
        "op_select": plant(jax.random.randint(splits[4], (BATCHES, N_SPACE, OB), 0, NH), jax.random.fold_in(splits[4], 1), 0, NH - 1).astype(jnp.int32),
        "op_table": scatter_about(splits[5], (NH, BLK, BLK), BLK ** -0.5, 0.5, (), jnp.float32),
        "loc_obs": plant(jax.random.randint(splits[6], (BATCHES, N_SPACE, NB, LOC), 0, 3 * OB), jax.random.fold_in(splits[6], 1), 0, (3 * OB) - 1).astype(jnp.int32),
        "loc_tile": plant(jax.random.randint(splits[7], (BATCHES, N_SPACE, NB, LOC), 0, NT), jax.random.fold_in(splits[7], 1), 0, NT - 1).astype(jnp.int32),
        "loc_tiles": jnp.clip(jax.random.uniform(splits[8], (NT, BLK, BLK), jnp.float32, 0.0, 1.0), 0.0, 1.0),
    }


def observe(blocks, obs_cell, op_select, op_table, batch_no):
    parts = []
    for slab_no in range(N_SPACE):
        picked = blocks[:, slab_no][:, obs_cell[batch_no, slab_no]]
        operators = op_table[op_select[batch_no, slab_no]]
        parts.append(jnp.einsum("koc,opc->kop", picked, operators, precision=lax.Precision.HIGHEST))
    return jnp.concatenate(parts, axis=1)


def reference(states, obs_values, obs_weights, obs_cell, op_select, op_table, loc_obs, loc_tile, loc_tiles):
    ensemble = states.reshape(K, N_SPACE, NB, BLK)
    for batch_no in range(BATCHES):
        observed = observe(ensemble, obs_cell, op_select, op_table, batch_no)
        obs_mean = jnp.mean(observed, axis=0)
        obs_anom = observed - obs_mean
        values = obs_values[batch_no].reshape(NOB, BLK)
        weights = obs_weights[batch_no].reshape(NOB, BLK)
        innov = weights * (values - obs_mean) - 0.5 * weights * obs_anom
        state_mean = jnp.mean(ensemble, axis=0)
        slabs = []
        for slab_no in range(N_SPACE):
            order = [(slab_no - 1) % N_SPACE, slab_no, (slab_no + 1) % N_SPACE]
            anom_win = jnp.concatenate([obs_anom[:, q * OB:(q + 1) * OB] for q in order], axis=1)
            innov_win = jnp.concatenate([innov[:, q * OB:(q + 1) * OB] for q in order], axis=1)

            def update_block(packed):
                cell_blk, mean_blk, reach, tile_pick = packed
                state_anom = cell_blk - mean_blk
                chosen = anom_win[:, reach]
                covariance = jnp.einsum("kc,klo->lco", state_anom, chosen, precision=lax.Precision.HIGHEST) / (K - 1)
                gain = loc_tiles[tile_pick] * covariance
                increment = jnp.einsum("klo,lco->kc", innov_win[:, reach], gain, precision=lax.Precision.HIGHEST)
                return cell_blk + increment

            fresh = lax.map(update_block, (ensemble[:, slab_no].transpose(1, 0, 2), state_mean[slab_no], loc_obs[batch_no, slab_no], loc_tile[batch_no, slab_no]))
            slabs.append(fresh.transpose(1, 0, 2))
        ensemble = jnp.stack(slabs, axis=1)
    return ensemble.reshape(K, NCELLS)
```

```python
import functools

import jax
import jax.numpy as jnp
from jax import lax
from jax.experimental import pallas as pl
from jax.experimental.pallas import tpu as pltpu
from jax.sharding import PartitionSpec as P

BLK = 128
NT_DIMS = (((1,), (1,)), ((), ()))


def split(x):
    hi = x.astype(jnp.bfloat16)
    lo = (x - hi.astype(jnp.float32)).astype(jnp.bfloat16)
    return hi, lo


def dot(a, b):
    return jnp.dot(a, b, preferred_element_type=jnp.float32)


def dot_nt(a, b):
    return lax.dot_general(a, b, NT_DIMS, preferred_element_type=jnp.float32)


def update_kernel(nb, ob, loc, picks, *refs):
    reach_ref, tile_ref, op_ref = refs[:3]
    refs = refs[3:]
    cells_ref, refs = refs[0], refs[1:]
    if picks:
        picked_ref, table_ref, refs = refs[0], refs[1], refs[2:]
    prev_ref, own_ref, next_ref, values_ref, weights_ref, tiles_ref = refs[:6]
    refs = refs[6:]
    out_ref, refs = refs[0], refs[1:]
    if picks:
        obs_ref, refs = refs[0], refs[1:]
    hi_ref, lo_ref, d_ref, acc_ref = refs
    members = cells_ref.shape[0]
    n = pl.program_id(0)

    @pl.when(n == 0)
    def _():
        for slab, ref in enumerate((prev_ref, own_ref, next_ref)):
            for o in range(ob):
                j = slab * ob + o
                block = ref[:, o * BLK:(o + 1) * BLK]
                mean = jnp.sum(block, axis=0, keepdims=True) * (1.0 / members)
                hi, lo = split(block - mean)
                hi_ref[j] = hi
                lo_ref[j] = lo
                d_ref[j] = weights_ref[j] * (values_ref[j] - mean)

    def update(cell):
        mean = jnp.sum(cell, axis=0, keepdims=True) * (1.0 / members)
        hi, lo = split(jnp.transpose(cell - mean))
        both = jnp.concatenate([hi, lo], axis=0)
        ones = []
        for pair in range(loc // 2):
            first, second = reach_ref[n, 2 * pair], reach_ref[n, 2 * pair + 1]
            obs_hi = jnp.concatenate([hi_ref[first], hi_ref[second]], axis=1)
            obs_lo = jnp.concatenate([lo_ref[first], lo_ref[second]], axis=1)
            part = dot(both, obs_hi)
            cov = part[:BLK] + part[BLK:] + dot(hi, obs_lo)
            tile = jnp.concatenate(
                [tiles_ref[tile_ref[n, 2 * pair]], tiles_ref[tile_ref[n, 2 * pair + 1]]], axis=1
            )
            gain = tile * (cov * (1.0 / (members - 1)))
            d = jnp.concatenate([d_ref[first], d_ref[second]], axis=1)
            w = jnp.concatenate([weights_ref[first], weights_ref[second]], axis=1)
            ones.append(jnp.sum(gain * d, axis=1, keepdims=True))
            gain_hi, gain_lo = split(gain * (-0.5 * w))
            step = dot_nt(obs_hi, jnp.concatenate([gain_hi, gain_lo], axis=0))
            step = step[:, :BLK] + step[:, BLK:] + dot_nt(obs_lo, gain_hi)
            if pair == 0:
                acc_ref[...] = step
            else:
                acc_ref[...] += step
        shift = functools.reduce(jnp.add, ones)
        row = jnp.transpose(jnp.broadcast_to(shift, (BLK, BLK)))[:1]
        return cell + (acc_ref[...] + row)

    if picks:
        @pl.when(n < nb)
        def _():
            out_ref[...] = update(cells_ref[...])

        @pl.when(n >= nb)
        def _():
            fresh_hi, fresh_lo = split(update(picked_ref[...]))
            op_hi, op_lo = split(table_ref[op_ref[jnp.maximum(n - nb, 0)]])
            part = dot_nt(fresh_hi, jnp.concatenate([op_hi, op_lo], axis=0))
            obs_ref[...] = part[:, :BLK] + part[:, BLK:] + dot_nt(fresh_lo, op_hi)
    else:
        out_ref[...] = update(cells_ref[...])


def update_cells(cells, window, values, weights, tiles, reach, tile_pick, picked=None, table=None, ops=None):
    members = cells.shape[0]
    nb = cells.shape[1] // BLK
    ob = window[0].shape[1] // BLK
    loc = reach.shape[1]
    picks = 0 if picked is None else ob
    whole = pl.BlockSpec(memory_space=pltpu.VMEM)
    block = pl.BlockSpec((members, BLK), lambda n, *_: (0, jnp.minimum(n, nb - 1)))
    late = pl.BlockSpec((members, BLK), lambda n, *_: (0, jnp.maximum(n - nb, 0)))
    if ops is None:
        ops = jnp.zeros((ob,), jnp.int32)
    args = [reach, tile_pick, ops, cells]
    in_specs = [block]
    out_shape = [jax.ShapeDtypeStruct(cells.shape, jnp.float32)]
    out_specs = [block]
    if picks:
        args += [picked, table]
        in_specs += [late, whole]
        out_shape.append(jax.ShapeDtypeStruct((members, ob * BLK), jnp.float32))
        out_specs.append(late)
    args += [*window, values, weights, tiles]
    in_specs += [whole] * 6
    return pl.pallas_call(
        functools.partial(update_kernel, nb, ob, loc, picks),
        grid_spec=pltpu.PrefetchScalarGridSpec(
            num_scalar_prefetch=3,
            grid=(nb + picks,),
            in_specs=in_specs,
            out_specs=out_specs,
            scratch_shapes=[
                pltpu.VMEM((3 * ob, members, BLK), jnp.bfloat16),
                pltpu.VMEM((3 * ob, members, BLK), jnp.bfloat16),
                pltpu.VMEM((3 * ob, 1, BLK), jnp.float32),
                pltpu.VMEM((members, BLK), jnp.float32),
            ],
        ),
        out_shape=out_shape,
        compiler_params=pltpu.CompilerParams(
            dimension_semantics=("arbitrary",), vmem_limit_bytes=56 * 1024 * 1024
        ),
    )(*args)


def window_values(flat_row, width):
    space_n = lax.axis_size("space")
    by_slab = flat_row.reshape(space_n, width)
    pick = (lax.axis_index("space") - 1 + jnp.arange(3, dtype=jnp.int32)) % space_n
    return by_slab[pick].reshape(3 * width // BLK, 1, BLK)


def halo(own):
    count = lax.axis_size("space")
    up = [(i, (i + 1) % count) for i in range(count)]
    down = [((i + 1) % count, i) for i in range(count)]
    return lax.ppermute(own, "space", up), own, lax.ppermute(own, "space", down)


def per_device(
    states, obs_values, obs_weights, obs_cell, op_select, op_table, loc_obs, loc_tile, loc_tiles
):
    share, width = states.shape
    ob = obs_cell.shape[2]
    obs_w = ob * BLK
    member_n = lax.axis_size("member")
    nb, loc = loc_obs.shape[2:]

    def pick(batch_no):
        return [
            lax.dynamic_slice_in_dim(states, obs_cell[batch_no, 0, o] * BLK, BLK, axis=1)
            for o in range(ob)
        ]

    first = jnp.stack(pick(0))
    observed = jnp.einsum(
        "okc,opc->kop", first, op_table[op_select[0, 0]], precision=lax.Precision.HIGHEST
    ).reshape(share, obs_w)
    second = jnp.concatenate(pick(1), axis=1)
    ints = jnp.stack([loc_obs[0, 0], loc_tile[0, 0]]).astype(jnp.float32).reshape(-1)
    extra = -(-ints.shape[0] // (2 * obs_w * 8)) * 8
    ints = jnp.pad(ints, (0, extra * 2 * obs_w - ints.shape[0])).reshape(extra, 2 * obs_w)
    sent = jnp.concatenate([jnp.concatenate([observed, second], axis=1), ints], axis=0)
    got = lax.all_gather(sent, "member", axis=0)
    own = got[:, :share, :obs_w].reshape(member_n * share, obs_w)
    picked = got[:, :share, obs_w:].reshape(member_n * share, obs_w)
    table = got[:, share:].reshape(member_n, -1)[:, : 2 * nb * loc]
    table = table.reshape(member_n, 2, nb, loc).astype(jnp.int32)
    table = table.transpose(1, 0, 2, 3).reshape(2, member_n * nb, loc)
    late = table[:, obs_cell[1, 0]]
    reach = jnp.concatenate([loc_obs[0, 0], late[0]], axis=0)
    tile_pick = jnp.concatenate([loc_tile[0, 0], late[1]], axis=0)

    cells = lax.all_to_all(states, "member", split_axis=1, concat_axis=0, tiled=True)
    cells, observed = update_cells(
        cells, halo(own), window_values(obs_values[0], obs_w), window_values(obs_weights[0], obs_w),
        loc_tiles, reach, tile_pick, picked, op_table, op_select[1, 0],
    )
    (cells,) = update_cells(
        cells, halo(observed), window_values(obs_values[1], obs_w),
        window_values(obs_weights[1], obs_w), loc_tiles, loc_obs[1, 0], loc_tile[1, 0],
    )
    return lax.all_to_all(cells, "member", split_axis=0, concat_axis=1, tiled=True)


def solution(mesh):
    placed = (
        P("member", "space"),
        P(),
        P(),
        P(None, "space", None),
        P(None, "space", None),
        P(),
        P(None, "space", "member", None),
        P(None, "space", "member", None),
        P(),
    )
    return jax.shard_map(
        per_device, mesh=mesh, in_specs=placed, out_specs=P("member", "space"), check_vma=False
    )
```

```python
import functools

import jax
import jax.numpy as jnp
from jax import lax
from jax.experimental import pallas as pl
from jax.experimental.pallas import tpu as pltpu
from jax.sharding import PartitionSpec as P

BLK = 128
NT_DIMS = (((1,), (1,)), ((), ()))


def split(x):
    hi = x.astype(jnp.bfloat16)
    lo = (x - hi.astype(jnp.float32)).astype(jnp.bfloat16)
    return hi, lo


def dot(a, b):
    return jnp.dot(a, b, preferred_element_type=jnp.float32)


def dot_nt(a, b):
    return lax.dot_general(a, b, NT_DIMS, preferred_element_type=jnp.float32)


def update_kernel(ob, loc, picks, *refs):
    reach_ref, tile_ref, op_ref = refs[:3]
    refs = refs[3:]
    cells_ref, refs = refs[0], refs[1:]
    if picks:
        table_ref, refs = refs[0], refs[1:]
    prev_ref, own_ref, next_ref, values_ref, weights_ref, tiles_ref = refs[:6]
    refs = refs[6:]
    out_ref, refs = refs[0], refs[1:]
    hi_ref, lo_ref, d_ref, acc_ref = refs
    members = cells_ref.shape[0]
    n = pl.program_id(0)

    @pl.when(n == 0)
    def _():
        for slab, ref in enumerate((prev_ref, own_ref, next_ref)):
            for o in range(ob):
                j = slab * ob + o
                block = ref[:, o * BLK:(o + 1) * BLK]
                mean = jnp.sum(block, axis=0, keepdims=True) * (1.0 / members)
                hi, lo = split(block - mean)
                hi_ref[j] = hi
                lo_ref[j] = lo
                d_ref[j] = weights_ref[j] * (values_ref[j] - mean)

    def update(cell):
        mean = jnp.sum(cell, axis=0, keepdims=True) * (1.0 / members)
        hi, lo = split(jnp.transpose(cell - mean))
        both = jnp.concatenate([hi, lo], axis=0)
        ones = []
        for pair in range(loc // 2):
            first, second = reach_ref[n, 2 * pair], reach_ref[n, 2 * pair + 1]
            obs_hi = jnp.concatenate([hi_ref[first], hi_ref[second]], axis=1)
            obs_lo = jnp.concatenate([lo_ref[first], lo_ref[second]], axis=1)
            part = dot(both, obs_hi)
            cov = part[:BLK] + part[BLK:] + dot(hi, obs_lo)
            tile = jnp.concatenate(
                [tiles_ref[tile_ref[n, 2 * pair]], tiles_ref[tile_ref[n, 2 * pair + 1]]], axis=1
            )
            gain = tile * (cov * (1.0 / (members - 1)))
            d = jnp.concatenate([d_ref[first], d_ref[second]], axis=1)
            w = jnp.concatenate([weights_ref[first], weights_ref[second]], axis=1)
            ones.append(jnp.sum(gain * d, axis=1, keepdims=True))
            gain_hi, gain_lo = split(gain * (-0.5 * w))
            step = dot_nt(obs_hi, jnp.concatenate([gain_hi, gain_lo], axis=0))
            step = step[:, :BLK] + step[:, BLK:] + dot_nt(obs_lo, gain_hi)
            if pair == 0:
                acc_ref[...] = step
            else:
                acc_ref[...] += step
        shift = functools.reduce(jnp.add, ones)
        row = jnp.transpose(jnp.broadcast_to(shift, (BLK, BLK)))[:1]
        return cell + (acc_ref[...] + row)

    if picks:
        fresh_hi, fresh_lo = split(update(cells_ref[...]))
        op_hi, op_lo = split(table_ref[op_ref[n]])
        part = dot_nt(fresh_hi, jnp.concatenate([op_hi, op_lo], axis=0))
        out_ref[...] = part[:, :BLK] + part[:, BLK:] + dot_nt(fresh_lo, op_hi)
    else:
        out_ref[...] = update(cells_ref[...])


def update_cells(cells, window, values, weights, tiles, reach, tile_pick, table=None, ops=None):
    members = cells.shape[0]
    nb = cells.shape[1] // BLK
    ob = window[0].shape[1] // BLK
    loc = reach.shape[1]
    picks = table is not None
    whole = pl.BlockSpec(memory_space=pltpu.VMEM)
    block = pl.BlockSpec((members, BLK), lambda n, *_: (0, n))
    if ops is None:
        ops = jnp.zeros((ob,), jnp.int32)
    args = [reach, tile_pick, ops, cells] + ([table] if picks else [])
    args += [*window, values, weights, tiles]
    return pl.pallas_call(
        functools.partial(update_kernel, ob, loc, picks),
        grid_spec=pltpu.PrefetchScalarGridSpec(
            num_scalar_prefetch=3,
            grid=(nb,),
            in_specs=[block] + [whole] * (len(args) - 4),
            out_specs=block,
            scratch_shapes=[
                pltpu.VMEM((3 * ob, members, BLK), jnp.bfloat16),
                pltpu.VMEM((3 * ob, members, BLK), jnp.bfloat16),
                pltpu.VMEM((3 * ob, 1, BLK), jnp.float32),
                pltpu.VMEM((members, BLK), jnp.float32),
            ],
        ),
        out_shape=jax.ShapeDtypeStruct(cells.shape, jnp.float32),
        compiler_params=pltpu.CompilerParams(
            dimension_semantics=("arbitrary",), vmem_limit_bytes=56 * 1024 * 1024
        ),
        cost_estimate=pl.CostEstimate(
            flops=16 * nb * members * BLK * BLK * loc, bytes_accessed=32 << 20, transcendentals=0
        ),
    )(*args)


def gather_kernel(member_n, space_n, *refs):
    ins, refs = refs[:3], refs[3:]
    outs, refs = refs[:3], refs[3:]
    prev_ref, next_ref, send_sem, recv_sem, halo_send, halo_recv, local_sem = refs
    me = lax.axis_index("member")
    slab = lax.axis_index("space")
    line = member_n // 2
    at, lane = me // 2, lax.rem(me, 2)
    mate = at * 2 + 1 - lane
    after = lax.rem(slab + 1, space_n)
    before = lax.rem(slab + space_n - 1, space_n)

    barrier = pltpu.get_barrier_semaphore()

    def greet(member, space):
        pl.semaphore_signal(
            barrier, inc=1, device_id=(member, space), device_id_type=pl.DeviceIdType.MESH
        )

    greet(mate, slab)
    greet(me, after)
    greet(me, before)

    @pl.when(at > 0)
    def _():
        greet(me - 2, slab)

    @pl.when(at < line - 1)
    def _():
        greet(me + 2, slab)

    pl.semaphore_wait(
        barrier, 3 + jnp.where(at > 0, 1, 0) + jnp.where(at < line - 1, 1, 0)
    )

    def rows(ref, item, block):
        size = ins[item].shape[0]
        return ref.at[pl.ds(pl.multiple_of(block * size, 8), size)]

    def hop(item, block, way, target, mine=False):
        return pltpu.make_async_remote_copy(
            src_ref=ins[item] if mine else rows(outs[item], item, block),
            dst_ref=rows(outs[item], item, block),
            send_sem=send_sem.at[item, block, way],
            recv_sem=recv_sem.at[item, block],
            device_id=(target, slab),
            device_id_type=pl.DeviceIdType.MESH,
        )

    def side(block, way, mine=False):
        return pltpu.make_async_remote_copy(
            src_ref=ins[0] if mine else rows(outs[0], 0, block),
            dst_ref=rows((prev_ref, next_ref)[way], 0, block),
            send_sem=halo_send.at[block, way],
            recv_sem=halo_recv.at[block, way],
            device_id=(me, (after, before)[way]),
            device_id_type=pl.DeviceIdType.MESH,
        )

    def sides(block, mine=False):
        side(block, 0, mine).start()
        side(block, 1, mine).start()

    for item in range(3):
        @pl.when(at < line - 1)
        def _():
            hop(item, me, 0, me + 2, True).start()

        @pl.when(at > 0)
        def _():
            hop(item, me, 1, me - 2, True).start()

        hop(item, me, 2, mate, True).start()
    sides(me, True)
    local = [
        pltpu.make_async_copy(ins[item], rows(outs[item], item, me), local_sem.at[item])
        for item in range(3)
    ]
    for copy in local:
        copy.start()

    def landed(item, block):
        hop(item, block, 2, mate).wait_recv()

    def from_mate(block):
        for item in range(3):
            landed(item, block)
            if item == 0:
                sides(block)

    for step in range(1, line):
        low, high = me - 2 * step, me + 2 * step

        @pl.when(low >= 0)
        def _():
            for item in range(3):
                landed(item, low)

                @pl.when(at < line - 1)
                def _():
                    hop(item, low, 0, me + 2).start()

                hop(item, low, 2, mate).start()
                if item == 0:
                    sides(low)

        @pl.when(high < member_n)
        def _():
            for item in range(3):
                landed(item, high)

                @pl.when(at > 0)
                def _():
                    hop(item, high, 1, me - 2).start()

                hop(item, high, 2, mate).start()
                if item == 0:
                    sides(high)

        if step == 1:
            from_mate(mate)
        else:
            @pl.when(mate - 2 * (step - 1) >= 0)
            def _():
                from_mate(mate - 2 * (step - 1))

            @pl.when(mate + 2 * (step - 1) < member_n)
            def _():
                from_mate(mate + 2 * (step - 1))

    @pl.when(mate - 2 * (line - 1) >= 0)
    def _():
        from_mate(mate - 2 * (line - 1))

    @pl.when(mate + 2 * (line - 1) < member_n)
    def _():
        from_mate(mate + 2 * (line - 1))

    for copy in local:
        copy.wait()
    for block in range(member_n):
        for way in range(2):
            side(block, way).wait()
        place, same = block // 2, block % 2 == lane
        for item in range(3):
            @pl.when(same & (place <= at) & (at < line - 1))
            def _():
                hop(item, block, 0, mate).wait_send()

            @pl.when(same & (place >= at) & (at > 0))
            def _():
                hop(item, block, 1, mate).wait_send()

            @pl.when(same)
            def _():
                hop(item, block, 2, mate).wait_send()


def gather(observed, picked, ints):
    member_n, space_n = lax.axis_size("member"), lax.axis_size("space")
    parts = (observed, picked, ints)
    out = [jax.ShapeDtypeStruct((member_n * a.shape[0], a.shape[1]), a.dtype) for a in parts]
    return pl.pallas_call(
        functools.partial(gather_kernel, member_n, space_n),
        out_shape=out + [out[0], out[0]],
        in_specs=[pl.BlockSpec(memory_space=pltpu.VMEM)] * 3,
        out_specs=[pl.BlockSpec(memory_space=pl.ANY)] * 5,
        scratch_shapes=[
            pltpu.SemaphoreType.DMA((3, member_n, 3)),
            pltpu.SemaphoreType.DMA((3, member_n)),
            pltpu.SemaphoreType.DMA((member_n, 2)),
            pltpu.SemaphoreType.DMA((member_n, 2)),
            pltpu.SemaphoreType.DMA((3,)),
        ],
        compiler_params=pltpu.CompilerParams(collective_id=0, has_side_effects=True),
    )(*parts)


def window_values(flat_row, width):
    space_n = lax.axis_size("space")
    by_slab = flat_row.reshape(space_n, width)
    pick = (lax.axis_index("space") - 1 + jnp.arange(3, dtype=jnp.int32)) % space_n
    return by_slab[pick].reshape(3 * width // BLK, 1, BLK)


def halo(own):
    count = lax.axis_size("space")
    up = [(i, (i + 1) % count) for i in range(count)]
    down = [((i + 1) % count, i) for i in range(count)]
    return lax.ppermute(own, "space", up), own, lax.ppermute(own, "space", down)


def per_device(
    states, obs_values, obs_weights, obs_cell, op_select, op_table, loc_obs, loc_tile, loc_tiles
):
    share, width = states.shape
    ob = obs_cell.shape[2]
    obs_w = ob * BLK
    member_n = lax.axis_size("member")
    nb, loc = loc_obs.shape[2:]

    def pick(batch_no):
        return [
            lax.dynamic_slice_in_dim(states, obs_cell[batch_no, 0, o] * BLK, BLK, axis=1)
            for o in range(ob)
        ]

    first = jnp.stack(pick(0))
    observed = jnp.einsum(
        "okc,opc->kop", first, op_table[op_select[0, 0]], precision=lax.Precision.HIGHEST
    ).reshape(share, obs_w)
    second = jnp.concatenate(pick(1), axis=1)
    ints = jnp.stack([loc_obs[0, 0], loc_tile[0, 0]]).astype(jnp.float32).reshape(-1)
    extra = -(-ints.shape[0] // (8 * BLK)) * 8
    ints = jnp.pad(ints, (0, extra * BLK - ints.shape[0])).reshape(extra, BLK)
    cells = lax.all_to_all(states, "member", split_axis=1, concat_axis=0, tiled=True)
    own, picked, table, before, after = gather(observed, second, ints)
    table = table.reshape(member_n, extra * BLK)[:, : 2 * nb * loc]
    table = table.reshape(member_n, 2, nb, loc).astype(jnp.int32)
    table = table.transpose(1, 0, 2, 3).reshape(2, member_n * nb, loc)
    late = table[:, obs_cell[1, 0]]

    values = [window_values(obs_values[b], obs_w) for b in range(2)]
    weights = [window_values(obs_weights[b], obs_w) for b in range(2)]
    window = (before, own, after)
    observed = update_cells(
        picked, window, values[0], weights[0], loc_tiles, late[0], late[1], op_table, op_select[1, 0]
    )
    cells = update_cells(
        cells, window, values[0], weights[0], loc_tiles, loc_obs[0, 0], loc_tile[0, 0]
    )
    cells = update_cells(
        cells, halo(observed), values[1], weights[1], loc_tiles, loc_obs[1, 0], loc_tile[1, 0]
    )
    return lax.all_to_all(cells, "member", split_axis=0, concat_axis=1, tiled=True)


def solution(mesh):
    placed = (
        P("member", "space"),
        P(),
        P(),
        P(None, "space", None),
        P(None, "space", None),
        P(),
        P(None, "space", "member", None),
        P(None, "space", "member", None),
        P(),
    )
    return jax.shard_map(
        per_device, mesh=mesh, in_specs=placed, out_specs=P("member", "space"), check_vma=False
    )
```

```python
import functools

import jax
import jax.numpy as jnp
from jax import lax
from jax.experimental import pallas as pl
from jax.experimental.pallas import tpu as pltpu
from jax.sharding import PartitionSpec as P

BLK = 128
NT_DIMS = (((1,), (1,)), ((), ()))


def split(x):
    hi = x.astype(jnp.bfloat16)
    lo = (x - hi.astype(jnp.float32)).astype(jnp.bfloat16)
    return hi, lo


def dot(a, b):
    return jnp.dot(a, b, preferred_element_type=jnp.float32)


def dot_nt(a, b):
    return lax.dot_general(a, b, NT_DIMS, preferred_element_type=jnp.float32)


def send(src, dst, send_sem, recv_sem, member, space):
    return pltpu.make_async_remote_copy(
        src_ref=src,
        dst_ref=dst,
        send_sem=send_sem,
        recv_sem=recv_sem,
        device_id=(member, space),
        device_id_type=pl.DeviceIdType.MESH,
    )


def columns(ref, block):
    return ref.at[:, pl.ds(pl.multiple_of(block * BLK, BLK), BLK)]


def ring_of_slabs(space_n):
    slab = lax.axis_index("space")
    return slab, lax.rem(slab + 1, space_n), lax.rem(slab + space_n - 1, space_n)


def load_window(batch_no, ob, space_n, window, values_ref, weights_ref, scratch):
    hi_ref, lo_ref, d_ref, w_ref = scratch[:4]
    members = window[0].shape[0]
    slab = lax.axis_index("space")
    for place, ref in enumerate(window):
        source = lax.rem(slab + space_n - 1 + place, space_n)
        for o in range(ob):
            j = place * ob + o
            row = (batch_no * space_n + source) * ob + o
            block = ref[:, o * BLK:(o + 1) * BLK]
            mean = jnp.sum(block, axis=0, keepdims=True) * (1.0 / members)
            hi, lo = split(block - mean)
            hi_ref[j] = hi
            lo_ref[j] = lo
            w_ref[j] = weights_ref[row]
            d_ref[j] = weights_ref[row] * (values_ref[row] - mean)


def update(cell, picks, tiles_ref, scratch):
    hi_ref, lo_ref, d_ref, w_ref, acc_ref = scratch
    members = cell.shape[0]
    mean = jnp.sum(cell, axis=0, keepdims=True) * (1.0 / members)
    hi, lo = split(jnp.transpose(cell - mean))
    both = jnp.concatenate([hi, lo], axis=0)
    ones = []
    for pair in range(len(picks) // 2):
        (first, tile_a), (second, tile_b) = picks[2 * pair], picks[2 * pair + 1]
        obs_hi = jnp.concatenate([hi_ref[first], hi_ref[second]], axis=1)
        obs_lo = jnp.concatenate([lo_ref[first], lo_ref[second]], axis=1)
        part = dot(both, obs_hi)
        cov = part[:BLK] + part[BLK:] + dot(hi, obs_lo)
        tile = jnp.concatenate([tiles_ref[tile_a], tiles_ref[tile_b]], axis=1)
        gain = tile * (cov * (1.0 / (members - 1)))
        d = jnp.concatenate([d_ref[first], d_ref[second]], axis=1)
        w = jnp.concatenate([w_ref[first], w_ref[second]], axis=1)
        ones.append(jnp.sum(gain * d, axis=1, keepdims=True))
        gain_hi, gain_lo = split(gain * (-0.5 * w))
        step = dot_nt(obs_hi, jnp.concatenate([gain_hi, gain_lo], axis=0))
        step = step[:, :BLK] + step[:, BLK:] + dot_nt(obs_lo, gain_hi)
        if pair == 0:
            acc_ref[...] = step
        else:
            acc_ref[...] += step
    shift = functools.reduce(jnp.add, ones)
    row = jnp.transpose(jnp.broadcast_to(shift, (BLK, BLK)))[:1]
    return cell + (acc_ref[...] + row)


def window_scratch(ob, members):
    return [
        pltpu.VMEM((3 * ob, members, BLK), jnp.bfloat16),
        pltpu.VMEM((3 * ob, members, BLK), jnp.bfloat16),
        pltpu.VMEM((3 * ob, 1, BLK), jnp.float32),
        pltpu.VMEM((3 * ob, 1, BLK), jnp.float32),
        pltpu.VMEM((members, BLK), jnp.float32),
    ]


def params(collective_id):
    return pltpu.CompilerParams(
        dimension_semantics=("arbitrary",),
        vmem_limit_bytes=56 * 1024 * 1024,
        collective_id=collective_id,
        has_side_effects=True,
    )


def cost(blocks, members, loc):
    return pl.CostEstimate(
        flops=16 * blocks * members * BLK * BLK * loc, bytes_accessed=32 << 20, transcendentals=0
    )


def first_kernel(nb, ob, loc, space_n, *refs):
    ints_ref, cell_ref, op_ref, reach_ref, tile_ref, picked_ref, cells_ref, table_ref = refs[:8]
    before_ref, own_ref, after_ref, values_ref, weights_ref, tiles_ref = refs[8:14]
    out_ref, obs_ref, prev_ref, next_ref = refs[14:18]
    scratch, (stage_ref, send_sem, recv_sem) = refs[18:23], refs[23:]
    n = pl.program_id(0)
    me = lax.axis_index("member")
    slab, after, before = ring_of_slabs(space_n)
    per_member = -(-2 * nb * loc // (8 * BLK)) * 8

    def side(block, way):
        return send(
            stage_ref.at[block],
            columns((prev_ref, next_ref)[way], block),
            send_sem.at[block, way],
            recv_sem.at[block, way],
            me,
            (after, before)[way],
        )

    @pl.when(n == 0)
    def _():
        barrier = pltpu.get_barrier_semaphore()
        for space in (after, before):
            pl.semaphore_signal(
                barrier, inc=1, device_id=(me, space), device_id_type=pl.DeviceIdType.MESH
            )
        pl.semaphore_wait(barrier, 2)
        load_window(0, ob, space_n, (before_ref, own_ref, after_ref), values_ref, weights_ref, scratch)

    @pl.when(n < ob)
    def _():
        cell = cell_ref[ob + n]
        owner = cell // nb

        def look(which, l):
            at = (which * nb + cell - owner * nb) * loc + l
            return ints_ref[owner * per_member + at // BLK, lax.rem(at, BLK)]

        picks = [(look(0, l), look(1, l)) for l in range(loc)]
        fresh_hi, fresh_lo = split(update(picked_ref[...], picks, tiles_ref, scratch))
        op_hi, op_lo = split(table_ref[op_ref[ob + n]])
        part = dot_nt(fresh_hi, jnp.concatenate([op_hi, op_lo], axis=0))
        part = part[:, :BLK] + part[:, BLK:] + dot_nt(fresh_lo, op_hi)
        obs_ref[...] = part
        stage_ref[n] = part
        side(n, 0).start()
        side(n, 1).start()

    @pl.when(n >= ob)
    def _():
        b = jnp.maximum(n - ob, 0)
        picks = [(reach_ref[b, l], tile_ref[b, l]) for l in range(loc)]
        out_ref[...] = update(cells_ref[...], picks, tiles_ref, scratch)

    @pl.when(n == ob + nb - 1)
    def _():
        for block in range(ob):
            side(block, 0).wait()
            side(block, 1).wait()


def first_batch(ints, cell, ops, reach, tile_pick, picked, cells, table, window, values, weights, tiles):
    members, wide = picked.shape
    nb, ob, loc = cells.shape[1] // BLK, wide // BLK, reach.shape[1]
    whole = pl.BlockSpec(memory_space=pltpu.VMEM)
    anywhere = pl.BlockSpec(memory_space=pl.ANY)
    early = pl.BlockSpec((members, BLK), lambda n, *_: (0, jnp.minimum(n, ob - 1)))
    late = pl.BlockSpec((members, BLK), lambda n, *_: (0, jnp.maximum(n - ob, 0)))
    seen = jax.ShapeDtypeStruct(picked.shape, jnp.float32)
    return pl.pallas_call(
        functools.partial(first_kernel, nb, ob, loc, lax.axis_size("space")),
        grid_spec=pltpu.PrefetchScalarGridSpec(
            num_scalar_prefetch=5,
            grid=(ob + nb,),
            in_specs=[early, late] + [whole] * 7,
            out_specs=[late, early, anywhere, anywhere],
            scratch_shapes=window_scratch(ob, members) + [
                pltpu.VMEM((ob, members, BLK), jnp.float32),
                pltpu.SemaphoreType.DMA((ob, 2)),
                pltpu.SemaphoreType.DMA((ob, 2)),
            ],
        ),
        out_shape=[jax.ShapeDtypeStruct(cells.shape, jnp.float32), seen, seen, seen],
        compiler_params=params(1),
        cost_estimate=cost(ob + nb, members, loc),
    )(ints, cell, ops, reach, tile_pick, picked, cells, table, *window, values, weights, tiles)


def last_kernel(nb, ob, loc, member_n, space_n, *refs):
    reach_ref, tile_ref, cells_ref, before_ref, own_ref, after_ref = refs[:6]
    values_ref, weights_ref, tiles_ref, out_ref = refs[6:10]
    scratch, (stage_ref, send_sem, recv_sem, local_sem) = refs[10:15], refs[15:]
    n = pl.program_id(0)
    me = lax.axis_index("member")
    slab = lax.axis_index("space")
    share = out_ref.shape[0]

    def part(block, member):
        return stage_ref.at[block, pl.ds(pl.multiple_of(member * share, 8), share)]

    def give(block, hop):
        peer = lax.rem(me + hop, member_n)
        return send(
            part(block, peer),
            columns(out_ref, me * nb + block),
            send_sem.at[block, hop],
            recv_sem.at[block, me],
            peer,
            slab,
        )

    def keep(block):
        return pltpu.make_async_copy(
            part(block, me), columns(out_ref, me * nb + block), local_sem.at[block]
        )

    @pl.when(n == 0)
    def _():
        barrier = pltpu.get_barrier_semaphore()
        for hop in range(1, member_n):
            peer = lax.rem(me + hop, member_n)
            pl.semaphore_signal(
                barrier, inc=1, device_id=(peer, slab), device_id_type=pl.DeviceIdType.MESH
            )
        pl.semaphore_wait(barrier, member_n - 1)
        load_window(1, ob, space_n, (before_ref, own_ref, after_ref), values_ref, weights_ref, scratch)

    picks = [(reach_ref[n, l], tile_ref[n, l]) for l in range(loc)]
    stage_ref[n] = update(cells_ref[...], picks, tiles_ref, scratch)
    for hop in range(1, member_n):
        give(n, hop).start()
    keep(n).start()

    @pl.when(n == nb - 1)
    def _():
        for block in range(nb):
            keep(block).wait()
            for hop in range(1, member_n):
                give(block, hop).wait_send()
                peer = lax.rem(me + hop, member_n)
                send(
                    part(block, peer),
                    columns(out_ref, peer * nb + block),
                    send_sem.at[block, hop],
                    recv_sem.at[block, peer],
                    peer,
                    slab,
                ).wait_recv()


def last_batch(reach, tile_pick, cells, window, values, weights, tiles):
    members, width = cells.shape
    nb, ob, loc = width // BLK, window[0].shape[1] // BLK, reach.shape[1]
    member_n = lax.axis_size("member")
    whole = pl.BlockSpec(memory_space=pltpu.VMEM)
    block = pl.BlockSpec((members, BLK), lambda n, *_: (0, n))
    return pl.pallas_call(
        functools.partial(last_kernel, nb, ob, loc, member_n, lax.axis_size("space")),
        grid_spec=pltpu.PrefetchScalarGridSpec(
            num_scalar_prefetch=2,
            grid=(nb,),
            in_specs=[block] + [whole] * 6,
            out_specs=pl.BlockSpec(memory_space=pl.ANY),
            scratch_shapes=window_scratch(ob, members) + [
                pltpu.VMEM((nb, members, BLK), jnp.float32),
                pltpu.SemaphoreType.DMA((nb, member_n)),
                pltpu.SemaphoreType.DMA((nb, member_n)),
                pltpu.SemaphoreType.DMA((nb,)),
            ],
        ),
        out_shape=jax.ShapeDtypeStruct((members // member_n, width * member_n), jnp.float32),
        compiler_params=params(2),
        cost_estimate=cost(nb, members, loc),
    )(reach, tile_pick, cells, *window, values, weights, tiles)


def pick_kernel(ob, cell_ref, op_ref, states_ref, op_block_ref, observed_ref, picked_ref):
    n = pl.program_id(0)

    @pl.when(n < ob)
    def _():
        observed_ref[...] = lax.dot_general(
            states_ref[...],
            op_block_ref[0],
            NT_DIMS,
            precision=lax.Precision.HIGHEST,
            preferred_element_type=jnp.float32,
        )

    @pl.when(n >= ob)
    def _():
        picked_ref[...] = states_ref[...]


def pick_blocks(cell, ops, states, table):
    share, ob = states.shape[0], cell.shape[0] // 2
    out = jax.ShapeDtypeStruct((share, ob * BLK), jnp.float32)
    return pl.pallas_call(
        functools.partial(pick_kernel, ob),
        grid_spec=pltpu.PrefetchScalarGridSpec(
            num_scalar_prefetch=2,
            grid=(2 * ob,),
            in_specs=[
                pl.BlockSpec((share, BLK), lambda n, cell, ops: (0, cell[n])),
                pl.BlockSpec((1, BLK, BLK), lambda n, cell, ops: (ops[n], 0, 0)),
            ],
            out_specs=[
                pl.BlockSpec((share, BLK), lambda n, *_: (0, jnp.minimum(n, ob - 1))),
                pl.BlockSpec((share, BLK), lambda n, *_: (0, jnp.maximum(n - ob, 0))),
            ],
        ),
        out_shape=[out, out],
    )(cell, ops, states, table)


def gather_kernel(member_n, space_n, *refs):
    ins, refs = refs[:3], refs[3:]
    outs, refs = refs[:3], refs[3:]
    prev_ref, next_ref, send_sem, recv_sem, halo_send, halo_recv, local_sem = refs
    me = lax.axis_index("member")
    slab = lax.axis_index("space")
    line = member_n // 2
    at, lane = me // 2, lax.rem(me, 2)
    mate = at * 2 + 1 - lane
    after = lax.rem(slab + 1, space_n)
    before = lax.rem(slab + space_n - 1, space_n)

    barrier = pltpu.get_barrier_semaphore()

    def greet(member, space):
        pl.semaphore_signal(
            barrier, inc=1, device_id=(member, space), device_id_type=pl.DeviceIdType.MESH
        )

    greet(mate, slab)
    greet(me, after)
    greet(me, before)

    @pl.when(at > 0)
    def _():
        greet(me - 2, slab)

    @pl.when(at < line - 1)
    def _():
        greet(me + 2, slab)

    pl.semaphore_wait(
        barrier, 3 + jnp.where(at > 0, 1, 0) + jnp.where(at < line - 1, 1, 0)
    )

    def rows(ref, item, block):
        size = ins[item].shape[0]
        return ref.at[pl.ds(pl.multiple_of(block * size, 8), size)]

    def hop(item, block, way, target, mine=False):
        return pltpu.make_async_remote_copy(
            src_ref=ins[item] if mine else rows(outs[item], item, block),
            dst_ref=rows(outs[item], item, block),
            send_sem=send_sem.at[item, block, way],
            recv_sem=recv_sem.at[item, block],
            device_id=(target, slab),
            device_id_type=pl.DeviceIdType.MESH,
        )

    def side(block, way, mine=False):
        return pltpu.make_async_remote_copy(
            src_ref=ins[0] if mine else rows(outs[0], 0, block),
            dst_ref=rows((prev_ref, next_ref)[way], 0, block),
            send_sem=halo_send.at[block, way],
            recv_sem=halo_recv.at[block, way],
            device_id=(me, (after, before)[way]),
            device_id_type=pl.DeviceIdType.MESH,
        )

    def sides(block, mine=False):
        side(block, 0, mine).start()
        side(block, 1, mine).start()

    for item in range(3):
        @pl.when(at < line - 1)
        def _():
            hop(item, me, 0, me + 2, True).start()

        @pl.when(at > 0)
        def _():
            hop(item, me, 1, me - 2, True).start()

        hop(item, me, 2, mate, True).start()
    sides(me, True)
    local = [
        pltpu.make_async_copy(ins[item], rows(outs[item], item, me), local_sem.at[item])
        for item in range(3)
    ]
    for copy in local:
        copy.start()

    def landed(item, block):
        hop(item, block, 2, mate).wait_recv()

    def from_mate(block):
        for item in range(3):
            landed(item, block)
            if item == 0:
                sides(block)

    for step in range(1, line):
        low, high = me - 2 * step, me + 2 * step

        @pl.when(low >= 0)
        def _():
            for item in range(3):
                landed(item, low)

                @pl.when(at < line - 1)
                def _():
                    hop(item, low, 0, me + 2).start()

                hop(item, low, 2, mate).start()
                if item == 0:
                    sides(low)

        @pl.when(high < member_n)
        def _():
            for item in range(3):
                landed(item, high)

                @pl.when(at > 0)
                def _():
                    hop(item, high, 1, me - 2).start()

                hop(item, high, 2, mate).start()
                if item == 0:
                    sides(high)

        if step == 1:
            from_mate(mate)
        else:
            @pl.when(mate - 2 * (step - 1) >= 0)
            def _():
                from_mate(mate - 2 * (step - 1))

            @pl.when(mate + 2 * (step - 1) < member_n)
            def _():
                from_mate(mate + 2 * (step - 1))

    @pl.when(mate - 2 * (line - 1) >= 0)
    def _():
        from_mate(mate - 2 * (line - 1))

    @pl.when(mate + 2 * (line - 1) < member_n)
    def _():
        from_mate(mate + 2 * (line - 1))

    for copy in local:
        copy.wait()
    for block in range(member_n):
        for way in range(2):
            side(block, way).wait()
        place, same = block // 2, block % 2 == lane
        for item in range(3):
            @pl.when(same & (place <= at) & (at < line - 1))
            def _():
                hop(item, block, 0, mate).wait_send()

            @pl.when(same & (place >= at) & (at > 0))
            def _():
                hop(item, block, 1, mate).wait_send()

            @pl.when(same)
            def _():
                hop(item, block, 2, mate).wait_send()


def gather(observed, picked, ints):
    member_n, space_n = lax.axis_size("member"), lax.axis_size("space")
    parts = (observed, picked, ints)
    out = [jax.ShapeDtypeStruct((member_n * a.shape[0], a.shape[1]), a.dtype) for a in parts]
    return pl.pallas_call(
        functools.partial(gather_kernel, member_n, space_n),
        out_shape=out + [out[0], out[0]],
        in_specs=[pl.BlockSpec(memory_space=pltpu.VMEM)] * 3,
        out_specs=[pl.BlockSpec(memory_space=pl.ANY)] * 5,
        scratch_shapes=[
            pltpu.SemaphoreType.DMA((3, member_n, 3)),
            pltpu.SemaphoreType.DMA((3, member_n)),
            pltpu.SemaphoreType.DMA((member_n, 2)),
            pltpu.SemaphoreType.DMA((member_n, 2)),
            pltpu.SemaphoreType.DMA((3,)),
        ],
        compiler_params=pltpu.CompilerParams(collective_id=0, has_side_effects=True),
    )(*parts)


def per_device(
    states, obs_values, obs_weights, obs_cell, op_select, op_table, loc_obs, loc_tile, loc_tiles
):
    nb, loc = loc_obs.shape[2:]
    cell, ops = obs_cell.reshape(-1), op_select.reshape(-1)
    values = obs_values.reshape(-1, 1, BLK)
    weights = obs_weights.reshape(-1, 1, BLK)
    ints = jnp.concatenate([loc_obs[0, 0], loc_tile[0, 0]]).reshape(-1)
    extra = -(-ints.shape[0] // (8 * BLK)) * 8
    ints = jnp.pad(ints, (0, extra * BLK - ints.shape[0])).reshape(extra, BLK)

    cells = lax.all_to_all(states, "member", split_axis=1, concat_axis=0, tiled=True)
    observed, picked = pick_blocks(cell, ops, states, op_table)
    own, picked, ints, before, after = gather(observed, picked, ints)
    cells, own, before, after = first_batch(
        ints, cell, ops, loc_obs[0, 0], loc_tile[0, 0], picked, cells, op_table,
        (before, own, after), values, weights, loc_tiles,
    )
    return last_batch(
        loc_obs[1, 0], loc_tile[1, 0], cells, (before, own, after), values, weights, loc_tiles
    )


def solution(mesh):
    placed = (
        P("member", "space"),
        P(),
        P(),
        P(None, "space", None),
        P(None, "space", None),
        P(),
        P(None, "space", "member", None),
        P(None, "space", "member", None),
        P(),
    )
    return jax.shard_map(
        per_device, mesh=mesh, in_specs=placed, out_specs=P("member", "space"), check_vma=False
    )
```

```python
import functools

import jax
import jax.numpy as jnp
from jax import lax
from jax.experimental import pallas as pl
from jax.experimental.pallas import tpu as pltpu
from jax.sharding import PartitionSpec as P

BLK = 128
NT_DIMS = (((1,), (1,)), ((), ()))


def split(x):
    hi = x.astype(jnp.bfloat16)
    lo = (x - hi.astype(jnp.float32)).astype(jnp.bfloat16)
    return hi, lo


def dot(a, b):
    return jnp.dot(a, b, preferred_element_type=jnp.float32)


def dot_nt(a, b):
    return lax.dot_general(a, b, NT_DIMS, preferred_element_type=jnp.float32)


def send(src, dst, send_sem, recv_sem, member, space):
    return pltpu.make_async_remote_copy(
        src_ref=src,
        dst_ref=dst,
        send_sem=send_sem,
        recv_sem=recv_sem,
        device_id=(member, space),
        device_id_type=pl.DeviceIdType.MESH,
    )


def columns(ref, block):
    return ref.at[:, pl.ds(pl.multiple_of(block * BLK, BLK), BLK)]


def ring_of_slabs(space_n):
    slab = lax.axis_index("space")
    return slab, lax.rem(slab + 1, space_n), lax.rem(slab + space_n - 1, space_n)


def load_window(batch_no, ob, space_n, window, values_ref, weights_ref, scratch):
    hi_ref, lo_ref, d_ref, w_ref = scratch[:4]
    members = window[0].shape[0]
    slab = lax.axis_index("space")
    for place, ref in enumerate(window):
        source = lax.rem(slab + space_n - 1 + place, space_n)
        for o in range(ob):
            j = place * ob + o
            row = (batch_no * space_n + source) * ob + o
            block = ref[:, o * BLK:(o + 1) * BLK]
            mean = jnp.sum(block, axis=0, keepdims=True) * (1.0 / members)
            hi, lo = split(block - mean)
            hi_ref[j] = hi
            lo_ref[j] = lo
            w_ref[j] = weights_ref[row]
            d_ref[j] = weights_ref[row] * (values_ref[row] - mean)


def update(cell, picks, tiles_ref, scratch):
    hi_ref, lo_ref, d_ref, w_ref, acc_ref = scratch
    members = cell.shape[0]
    mean = jnp.sum(cell, axis=0, keepdims=True) * (1.0 / members)
    hi, lo = split(jnp.transpose(cell - mean))
    both = jnp.concatenate([hi, lo], axis=0)
    ones = []
    for pair in range(len(picks) // 2):
        (first, tile_a), (second, tile_b) = picks[2 * pair], picks[2 * pair + 1]
        obs_hi = jnp.concatenate([hi_ref[first], hi_ref[second]], axis=1)
        obs_lo = jnp.concatenate([lo_ref[first], lo_ref[second]], axis=1)
        part = dot(both, obs_hi)
        cov = part[:BLK] + part[BLK:] + dot(hi, obs_lo)
        tile = jnp.concatenate([tiles_ref[tile_a], tiles_ref[tile_b]], axis=1)
        gain = tile * (cov * (1.0 / (members - 1)))
        d = jnp.concatenate([d_ref[first], d_ref[second]], axis=1)
        w = jnp.concatenate([w_ref[first], w_ref[second]], axis=1)
        ones.append(jnp.sum(gain * d, axis=1, keepdims=True))
        gain_hi, gain_lo = split(gain * (-0.5 * w))
        step = dot_nt(obs_hi, jnp.concatenate([gain_hi, gain_lo], axis=0))
        step = step[:, :BLK] + step[:, BLK:] + dot_nt(obs_lo, gain_hi)
        if pair == 0:
            acc_ref[...] = step
        else:
            acc_ref[...] += step
    shift = functools.reduce(jnp.add, ones)
    row = jnp.transpose(jnp.broadcast_to(shift, (BLK, BLK)))[:1]
    return cell + (acc_ref[...] + row)


def window_scratch(ob, members):
    return [
        pltpu.VMEM((3 * ob, members, BLK), jnp.bfloat16),
        pltpu.VMEM((3 * ob, members, BLK), jnp.bfloat16),
        pltpu.VMEM((3 * ob, 1, BLK), jnp.float32),
        pltpu.VMEM((3 * ob, 1, BLK), jnp.float32),
        pltpu.VMEM((members, BLK), jnp.float32),
    ]


def params(collective_id):
    return pltpu.CompilerParams(
        dimension_semantics=("arbitrary",),
        vmem_limit_bytes=56 * 1024 * 1024,
        collective_id=collective_id,
        has_side_effects=True,
    )


def cost(blocks, members, loc):
    return pl.CostEstimate(
        flops=16 * blocks * members * BLK * BLK * loc, bytes_accessed=32 << 20, transcendentals=0
    )


def first_kernel(nb, ob, loc, space_n, *refs):
    ints_ref, cell_ref, op_ref, reach_ref, tile_ref, picked_ref, cells_ref, table_ref = refs[:8]
    before_ref, own_ref, after_ref, values_ref, weights_ref, tiles_ref = refs[8:14]
    out_ref, obs_ref, prev_ref, next_ref = refs[14:18]
    scratch, (stage_ref, send_sem, recv_sem) = refs[18:23], refs[23:]
    n = pl.program_id(0)
    me = lax.axis_index("member")
    slab, after, before = ring_of_slabs(space_n)
    per_member = -(-2 * nb * loc // (8 * BLK)) * 8

    def side(block, way):
        return send(
            stage_ref.at[block],
            columns((prev_ref, next_ref)[way], block),
            send_sem.at[block, way],
            recv_sem.at[block, way],
            me,
            (after, before)[way],
        )

    @pl.when(n == 0)
    def _():
        barrier = pltpu.get_barrier_semaphore()
        for space in (after, before):
            pl.semaphore_signal(
                barrier, inc=1, device_id=(me, space), device_id_type=pl.DeviceIdType.MESH
            )
        pl.semaphore_wait(barrier, 2)
        load_window(0, ob, space_n, (before_ref, own_ref, after_ref), values_ref, weights_ref, scratch)

    @pl.when(n < ob)
    def _():
        cell = cell_ref[ob + n]
        owner = cell // nb

        def look(which, l):
            at = (which * nb + cell - owner * nb) * loc + l
            return ints_ref[owner * per_member + at // BLK, lax.rem(at, BLK)]

        picks = [(look(0, l), look(1, l)) for l in range(loc)]
        fresh_hi, fresh_lo = split(update(picked_ref[...], picks, tiles_ref, scratch))
        op_hi, op_lo = split(table_ref[op_ref[ob + n]])
        part = dot_nt(fresh_hi, jnp.concatenate([op_hi, op_lo], axis=0))
        part = part[:, :BLK] + part[:, BLK:] + dot_nt(fresh_lo, op_hi)
        obs_ref[...] = part
        stage_ref[n] = part
        side(n, 0).start()
        side(n, 1).start()

    @pl.when(n >= ob)
    def _():
        b = jnp.maximum(n - ob, 0)
        picks = [(reach_ref[b, l], tile_ref[b, l]) for l in range(loc)]
        out_ref[...] = update(cells_ref[...], picks, tiles_ref, scratch)

    @pl.when(n == ob + nb - 1)
    def _():
        for block in range(ob):
            side(block, 0).wait()
            side(block, 1).wait()


def first_batch(ints, cell, ops, reach, tile_pick, picked, cells, table, window, values, weights, tiles):
    members, wide = picked.shape
    nb, ob, loc = cells.shape[1] // BLK, wide // BLK, reach.shape[1]
    whole = pl.BlockSpec(memory_space=pltpu.VMEM)
    anywhere = pl.BlockSpec(memory_space=pl.ANY)
    early = pl.BlockSpec((members, BLK), lambda n, *_: (0, jnp.minimum(n, ob - 1)))
    late = pl.BlockSpec((members, BLK), lambda n, *_: (0, jnp.maximum(n - ob, 0)))
    seen = jax.ShapeDtypeStruct(picked.shape, jnp.float32)
    return pl.pallas_call(
        functools.partial(first_kernel, nb, ob, loc, lax.axis_size("space")),
        grid_spec=pltpu.PrefetchScalarGridSpec(
            num_scalar_prefetch=5,
            grid=(ob + nb,),
            in_specs=[early, late] + [whole] * 7,
            out_specs=[late, early, anywhere, anywhere],
            scratch_shapes=window_scratch(ob, members) + [
                pltpu.VMEM((ob, members, BLK), jnp.float32),
                pltpu.SemaphoreType.DMA((ob, 2)),
                pltpu.SemaphoreType.DMA((ob, 2)),
            ],
        ),
        out_shape=[jax.ShapeDtypeStruct(cells.shape, jnp.float32), seen, seen, seen],
        compiler_params=params(1),
        cost_estimate=cost(ob + nb, members, loc),
    )(ints, cell, ops, reach, tile_pick, picked, cells, table, *window, values, weights, tiles)


def last_kernel(nb, ob, loc, member_n, space_n, *refs):
    reach_ref, tile_ref, cells_ref, before_ref, own_ref, after_ref = refs[:6]
    values_ref, weights_ref, tiles_ref, out_ref = refs[6:10]
    scratch, (stage_ref, send_sem, recv_sem, local_sem) = refs[10:15], refs[15:]
    n = pl.program_id(0)
    me = lax.axis_index("member")
    slab = lax.axis_index("space")
    share = out_ref.shape[0]

    def part(block, member):
        return stage_ref.at[block, pl.ds(pl.multiple_of(member * share, 8), share)]

    def give(block, hop):
        peer = lax.rem(me + hop, member_n)
        return send(
            part(block, peer),
            columns(out_ref, me * nb + block),
            send_sem.at[block, hop],
            recv_sem.at[block, me],
            peer,
            slab,
        )

    def keep(block):
        return pltpu.make_async_copy(
            part(block, me), columns(out_ref, me * nb + block), local_sem.at[block]
        )

    @pl.when(n == 0)
    def _():
        barrier = pltpu.get_barrier_semaphore()
        for hop in range(1, member_n):
            peer = lax.rem(me + hop, member_n)
            pl.semaphore_signal(
                barrier, inc=1, device_id=(peer, slab), device_id_type=pl.DeviceIdType.MESH
            )
        pl.semaphore_wait(barrier, member_n - 1)
        load_window(1, ob, space_n, (before_ref, own_ref, after_ref), values_ref, weights_ref, scratch)

    picks = [(reach_ref[n, l], tile_ref[n, l]) for l in range(loc)]
    stage_ref[n] = update(cells_ref[...], picks, tiles_ref, scratch)
    for hop in range(1, member_n):
        give(n, hop).start()
    keep(n).start()

    @pl.when(n == nb - 1)
    def _():
        for block in range(nb):
            keep(block).wait()
            for hop in range(1, member_n):
                give(block, hop).wait_send()
                peer = lax.rem(me + hop, member_n)
                send(
                    part(block, peer),
                    columns(out_ref, peer * nb + block),
                    send_sem.at[block, hop],
                    recv_sem.at[block, peer],
                    peer,
                    slab,
                ).wait_recv()


def last_batch(reach, tile_pick, cells, window, values, weights, tiles):
    members, width = cells.shape
    nb, ob, loc = width // BLK, window[0].shape[1] // BLK, reach.shape[1]
    member_n = lax.axis_size("member")
    whole = pl.BlockSpec(memory_space=pltpu.VMEM)
    block = pl.BlockSpec((members, BLK), lambda n, *_: (0, n))
    return pl.pallas_call(
        functools.partial(last_kernel, nb, ob, loc, member_n, lax.axis_size("space")),
        grid_spec=pltpu.PrefetchScalarGridSpec(
            num_scalar_prefetch=2,
            grid=(nb,),
            in_specs=[block] + [whole] * 6,
            out_specs=pl.BlockSpec(memory_space=pl.ANY),
            scratch_shapes=window_scratch(ob, members) + [
                pltpu.VMEM((nb, members, BLK), jnp.float32),
                pltpu.SemaphoreType.DMA((nb, member_n)),
                pltpu.SemaphoreType.DMA((nb, member_n)),
                pltpu.SemaphoreType.DMA((nb,)),
            ],
        ),
        out_shape=jax.ShapeDtypeStruct((members // member_n, width * member_n), jnp.float32),
        compiler_params=params(2),
        cost_estimate=cost(nb, members, loc),
    )(reach, tile_pick, cells, *window, values, weights, tiles)


def pick_kernel(ob, cell_ref, op_ref, states_ref, op_block_ref, observed_ref, picked_ref):
    n = pl.program_id(0)

    @pl.when(n < ob)
    def _():
        observed_ref[...] = lax.dot_general(
            states_ref[...],
            op_block_ref[0],
            NT_DIMS,
            precision=lax.Precision.HIGHEST,
            preferred_element_type=jnp.float32,
        )

    @pl.when(n >= ob)
    def _():
        picked_ref[...] = states_ref[...]


def pick_blocks(cell, ops, states, table):
    share, ob = states.shape[0], cell.shape[0] // 2
    out = jax.ShapeDtypeStruct((share, ob * BLK), jnp.float32)
    return pl.pallas_call(
        functools.partial(pick_kernel, ob),
        grid_spec=pltpu.PrefetchScalarGridSpec(
            num_scalar_prefetch=2,
            grid=(2 * ob,),
            in_specs=[
                pl.BlockSpec((share, BLK), lambda n, cell, ops: (0, cell[n])),
                pl.BlockSpec((1, BLK, BLK), lambda n, cell, ops: (ops[n], 0, 0)),
            ],
            out_specs=[
                pl.BlockSpec((share, BLK), lambda n, *_: (0, jnp.minimum(n, ob - 1))),
                pl.BlockSpec((share, BLK), lambda n, *_: (0, jnp.maximum(n - ob, 0))),
            ],
        ),
        out_shape=[out, out],
    )(cell, ops, states, table)


def gather_kernel(member_n, space_n, *refs):
    ins, states_ref, refs = refs[:3], refs[3], refs[4:]
    outs, refs = refs[:3], refs[3:]
    prev_ref, next_ref, cells_ref, send_sem, recv_sem, halo_send, halo_recv, local_sem = refs[:8]
    swap_send, swap_recv = refs[8:]
    share, width = states_ref.shape[0], cells_ref.shape[1]
    me = lax.axis_index("member")
    slab = lax.axis_index("space")
    line = member_n // 2
    at, lane = me // 2, lax.rem(me, 2)
    mate = at * 2 + 1 - lane
    after = lax.rem(slab + 1, space_n)
    before = lax.rem(slab + space_n - 1, space_n)

    barrier = pltpu.get_barrier_semaphore()

    def greet(member, space):
        pl.semaphore_signal(
            barrier, inc=1, device_id=(member, space), device_id_type=pl.DeviceIdType.MESH
        )

    greet(me, after)
    greet(me, before)
    for hop_by in range(1, member_n):
        greet(lax.rem(me + hop_by, member_n), slab)
    pl.semaphore_wait(barrier, member_n + 1)

    def states_for(member):
        return states_ref.at[:, pl.ds(pl.multiple_of(member * width, BLK), width)]

    def cells_of(member):
        return cells_ref.at[pl.ds(pl.multiple_of(member * share, 8), share)]

    def swap(hop_by):
        peer = lax.rem(me + hop_by, member_n)
        return send(
            states_for(peer), cells_of(me), swap_send.at[hop_by], swap_recv.at[me], peer, slab
        )

    hops = sorted(range(1, member_n), key=lambda k: (abs(k - line), k))
    each = -(-len(hops) // line)

    def swaps(step):
        for hop_by in hops[step * each:(step + 1) * each]:
            swap(hop_by).start()

    def rows(ref, item, block):
        size = ins[item].shape[0]
        return ref.at[pl.ds(pl.multiple_of(block * size, 8), size)]

    def hop(item, block, way, target, mine=False):
        return pltpu.make_async_remote_copy(
            src_ref=ins[item] if mine else rows(outs[item], item, block),
            dst_ref=rows(outs[item], item, block),
            send_sem=send_sem.at[item, block, way],
            recv_sem=recv_sem.at[item, block],
            device_id=(target, slab),
            device_id_type=pl.DeviceIdType.MESH,
        )

    def side(block, way, mine=False):
        return pltpu.make_async_remote_copy(
            src_ref=ins[0] if mine else rows(outs[0], 0, block),
            dst_ref=rows((prev_ref, next_ref)[way], 0, block),
            send_sem=halo_send.at[block, way],
            recv_sem=halo_recv.at[block, way],
            device_id=(me, (after, before)[way]),
            device_id_type=pl.DeviceIdType.MESH,
        )

    def sides(block, mine=False):
        side(block, 0, mine).start()
        side(block, 1, mine).start()

    for item in range(3):
        @pl.when(at < line - 1)
        def _():
            hop(item, me, 0, me + 2, True).start()

        @pl.when(at > 0)
        def _():
            hop(item, me, 1, me - 2, True).start()

        hop(item, me, 2, mate, True).start()
    sides(me, True)
    local = [
        pltpu.make_async_copy(ins[item], rows(outs[item], item, me), local_sem.at[item])
        for item in range(3)
    ]
    kept = pltpu.make_async_copy(states_for(me), cells_of(me), local_sem.at[3])
    swaps(0)
    for copy in local + [kept]:
        copy.start()

    def landed(item, block):
        hop(item, block, 2, mate).wait_recv()

    def from_mate(block):
        for item in range(3):
            landed(item, block)
            if item == 0:
                sides(block)

    for step in range(1, line):
        low, high = me - 2 * step, me + 2 * step

        @pl.when(low >= 0)
        def _():
            for item in range(3):
                landed(item, low)

                @pl.when(at < line - 1)
                def _():
                    hop(item, low, 0, me + 2).start()

                hop(item, low, 2, mate).start()
                if item == 0:
                    sides(low)

        @pl.when(high < member_n)
        def _():
            for item in range(3):
                landed(item, high)

                @pl.when(at > 0)
                def _():
                    hop(item, high, 1, me - 2).start()

                hop(item, high, 2, mate).start()
                if item == 0:
                    sides(high)

        swaps(step)
        if step == 1:
            from_mate(mate)
        else:
            @pl.when(mate - 2 * (step - 1) >= 0)
            def _():
                from_mate(mate - 2 * (step - 1))

            @pl.when(mate + 2 * (step - 1) < member_n)
            def _():
                from_mate(mate + 2 * (step - 1))

    @pl.when(mate - 2 * (line - 1) >= 0)
    def _():
        from_mate(mate - 2 * (line - 1))

    @pl.when(mate + 2 * (line - 1) < member_n)
    def _():
        from_mate(mate + 2 * (line - 1))

    for copy in local + [kept]:
        copy.wait()
    for hop_by in range(1, member_n):
        swap(hop_by).wait_send()
        peer = lax.rem(me + hop_by, member_n)
        send(
            states_for(peer), cells_of(peer), swap_send.at[hop_by], swap_recv.at[peer], peer, slab
        ).wait_recv()
    for block in range(member_n):
        for way in range(2):
            side(block, way).wait()
        place, same = block // 2, block % 2 == lane
        for item in range(3):
            @pl.when(same & (place <= at) & (at < line - 1))
            def _():
                hop(item, block, 0, mate).wait_send()

            @pl.when(same & (place >= at) & (at > 0))
            def _():
                hop(item, block, 1, mate).wait_send()

            @pl.when(same)
            def _():
                hop(item, block, 2, mate).wait_send()


def gather(observed, picked, ints, states):
    member_n, space_n = lax.axis_size("member"), lax.axis_size("space")
    parts = (observed, picked, ints)
    out = [jax.ShapeDtypeStruct((member_n * a.shape[0], a.shape[1]), a.dtype) for a in parts]
    share, width = states.shape
    cells = jax.ShapeDtypeStruct((share * member_n, width // member_n), states.dtype)
    return pl.pallas_call(
        functools.partial(gather_kernel, member_n, space_n),
        out_shape=out + [out[0], out[0], cells],
        in_specs=[pl.BlockSpec(memory_space=pltpu.VMEM)] * 3 + [pl.BlockSpec(memory_space=pl.ANY)],
        out_specs=[pl.BlockSpec(memory_space=pl.ANY)] * 6,
        scratch_shapes=[
            pltpu.SemaphoreType.DMA((3, member_n, 3)),
            pltpu.SemaphoreType.DMA((3, member_n)),
            pltpu.SemaphoreType.DMA((member_n, 2)),
            pltpu.SemaphoreType.DMA((member_n, 2)),
            pltpu.SemaphoreType.DMA((4,)),
            pltpu.SemaphoreType.DMA((member_n,)),
            pltpu.SemaphoreType.DMA((member_n,)),
        ],
        compiler_params=pltpu.CompilerParams(collective_id=0, has_side_effects=True),
    )(*parts, states)


def per_device(
    states, obs_values, obs_weights, obs_cell, op_select, op_table, loc_obs, loc_tile, loc_tiles
):
    nb, loc = loc_obs.shape[2:]
    cell, ops = obs_cell.reshape(-1), op_select.reshape(-1)
    values = obs_values.reshape(-1, 1, BLK)
    weights = obs_weights.reshape(-1, 1, BLK)
    ints = jnp.concatenate([loc_obs[0, 0], loc_tile[0, 0]]).reshape(-1)
    extra = -(-ints.shape[0] // (8 * BLK)) * 8
    ints = jnp.pad(ints, (0, extra * BLK - ints.shape[0])).reshape(extra, BLK)

    observed, picked = pick_blocks(cell, ops, states, op_table)
    own, picked, ints, before, after, cells = gather(observed, picked, ints, states)
    cells, own, before, after = first_batch(
        ints, cell, ops, loc_obs[0, 0], loc_tile[0, 0], picked, cells, op_table,
        (before, own, after), values, weights, loc_tiles,
    )
    return last_batch(
        loc_obs[1, 0], loc_tile[1, 0], cells, (before, own, after), values, weights, loc_tiles
    )


def solution(mesh):
    placed = (
        P("member", "space"),
        P(),
        P(),
        P(None, "space", None),
        P(None, "space", None),
        P(),
        P(None, "space", "member", None),
        P(None, "space", "member", None),
        P(),
    )
    return jax.shard_map(
        per_device, mesh=mesh, in_specs=placed, out_specs=P("member", "space"), check_vma=False
    )
```
